768 devices in a mesh: row: 16 (over z_hi, x, core), col: 48 (over z_lo, y).
Axes of the slice: x: 4, y: 8, z: 12 (z_hi: 2, z_lo: 6; z = z_hi * 6 + z_lo), core: 2. Of those that a mesh axis runs over, the one named last changes fastest.
Arguments:
- amplitudes: float32 [24576, 24576], P('row', 'col'), may hold values from -6 to 6
- intermediates: float32 [1152, 24576], P('row', 'col'), may hold values from -0.078125 to 0.078125
- integrals: float32 [24576, 1152], P(('row', 'col')), may hold values from -6 to 6
- row_pairs: int32 [2, 24576], P(None, ('row', 'col')), may hold values from 0 to 383, as said below
- window_virtuals: int32 [18], replicated, may hold values from 0 to 383, as said below
- occupied_energies: float32 [64], replicated, may hold values from -2 to -0.3
- virtual_energies: float32 [384], replicated, may hold values from 0.5 to 3
Outputs:
- update: float32 [24576, 1152], P(('row', 'col'))
The draws below stay inside these ranges and needn't reach their ends.
Inputs may be any that keep to these rules, and one draw needn't show every extreme that they name: `row_pairs`: every pair (a, i) with a < 384 and i < 64 stands in exactly one column. `window_virtuals`: 18 distinct virtual orbitals.
All inputs are finite; a program needn't handle non-finite values.
Results may differ from the reference program's by a relative error of at most 0.000062.
Values sent between devices are 32-bit elements; how exact they have to be, the bound alone decides.
A program may use at most 64 MiB of HBM per device.

```python
import jax
import jax.numpy as jnp
from jax import lax

NV = 384
NO = 64
NB = 18
NPH = 24576
NCOL = 1152


def draw_row_pairs(key, part):
    ordering = jax.random.permutation(key, NV * NO)
    return jnp.stack([ordering // NO, ordering % NO]).astype(jnp.int32)


def draw_window_virtuals(key, part):
    middle = jax.random.permutation(jax.random.fold_in(key, 1), NV - 2)[:NB - 2] + 1
    chosen = jnp.concatenate([jnp.array([0, NV - 1], dtype=jnp.int32), middle.astype(jnp.int32)])
    return jax.random.permutation(jax.random.fold_in(key, 2), chosen).astype(jnp.int32)


def levels(key, dims, cuts, low, largest):
    def one(position, shards_of):
        steps = jax.random.uniform(jax.random.fold_in(jax.random.fold_in(key, 6), position), (shards_of,), jnp.float32, low / len(cuts), largest / len(cuts))
        return jnp.repeat(jnp.exp(steps), dims[position] // shards_of).reshape((-1,) + (1,) * (len(dims) - position - 1))

    loudness = one(*cuts[0])
    for cut in cuts[1:]:
        loudness = loudness * one(*cut)
    return loudness


def scatter_about(key, extent, deviation, most, cuts=(), kind=jnp.bfloat16):
    factor_of = levels(key, extent, cuts, -0.22, 0.18) if cuts else 1.0
    entries = jax.random.normal(key, extent, jnp.float32) * deviation * factor_of
    return jnp.minimum(jnp.maximum(entries, -most), most).astype(kind)


def setup_inputs(seed: int = 0) -> dict:
    streams_of = jax.random.split(jax.random.key(seed), 8)
    amplitudes = scatter_about(streams_of[0], (NPH, NPH), 1.0, 6.0, ((0, 16), (1, 48)), jnp.float32)
    intermediates = scatter_about(streams_of[1], (NCOL, NPH), (NPH // 4) ** -0.5, 0.078125, ((0, 16), (1, 48)), jnp.float32)
    integrals = scatter_about(streams_of[2], (NPH, NCOL), 1.0, 6.0, ((0, 768),), jnp.float32)
    row_pairs = draw_row_pairs(jax.random.fold_in(streams_of[7], 71), 0)
    window_virtuals = draw_window_virtuals(jax.random.fold_in(streams_of[7], 71), 0)
    occupied_energies = jnp.clip(jax.random.uniform(streams_of[5], (NO,), jnp.float32, -2.0, -0.3), -2.0, -0.3)
    virtual_energies = jnp.clip(jax.random.uniform(streams_of[6], (NV,), jnp.float32, 0.5, 3.0), 0.5, 3.0)
    return dict(amplitudes=amplitudes, intermediates=intermediates, integrals=integrals, row_pairs=row_pairs, window_virtuals=window_virtuals, occupied_energies=occupied_energies, virtual_energies=virtual_energies)


def reference(amplitudes, intermediates, integrals, row_pairs, window_virtuals, occupied_energies, virtual_energies):
    cycle_term = jnp.dot(amplitudes, intermediates.T, precision=lax.Precision.HIGHEST, preferred_element_type=jnp.float32)
    gap_row = virtual_energies[row_pairs[0]] - occupied_energies[row_pairs[1]]
    window_energy = virtual_energies[window_virtuals]
    gap_col = (window_energy[:, None] - occupied_energies[None, :]).reshape(NCOL)
    return (integrals + cycle_term) / (gap_row[:, None] + gap_col[None, :])
```

```python
import functools

import jax
import jax.numpy as jnp
from jax import lax
from jax.experimental import pallas as pl
from jax.experimental.pallas import tpu as pltpu
from jax.sharding import PartitionSpec as P

MESH = pl.DeviceIdType.MESH
NX, NY, NZ, NL = 4, 8, 12, 6
RB = 32
DEPTH = 512
WIN = 72
CW = 384
NCOL = 1152


def lookup_table(indices, table):
    positions = lax.broadcasted_iota(jnp.int32, (indices.shape[0], table.shape[0]), 1)
    matches = indices[:, None] == positions
    return jnp.sum(jnp.where(matches, table[None, :], jnp.float32(0.0)), axis=1)


def split_hi_lo(value):
    hi = value.astype(jnp.bfloat16)
    return hi, (value - hi.astype(jnp.float32)).astype(jnp.bfloat16)


def kernel(
    a_hbm,
    b_ref,
    out_ref,
    a_vmem,
    a_hi,
    a_lo,
    gathered,
    relay,
    b_hi,
    b_lo,
    ybuf,
    ypart,
    zup,
    zdown,
    zpart,
    wup,
    wdown,
    usum,
    ubuf,
    a_sem,
    g_send,
    g_recv,
    y_send,
    y_recv,
    z_send,
    z_recv,
    w_send,
    w_recv,
    u_send,
    u_recv,
):
    row, col = lax.axis_index("row"), lax.axis_index("col")
    core = lax.rem(row, 2)
    x = lax.rem(lax.div(row, 2), NX)
    zhi = lax.div(row, 2 * NX)
    y = lax.rem(col, NY)
    i = lax.div(col, NY)
    z = zhi * NL + i
    sign = 1 - 2 * core

    def place(zhi_, x_, core_):
        return (zhi_ * NX + x_) * 2 + core_

    def device(x_, y_, z_, core_):
        return {
            "row": place(lax.div(z_, NL), x_, core_),
            "col": lax.rem(z_, NL) * NY + y_,
        }

    def at_x(step):
        return device(lax.rem(x + step + NX, NX), y, z, core)

    def at_y(step):
        return device(x, lax.rem(y + step + NY, NY), z, core)

    def at_z(step):
        return device(x, y, lax.rem(z + step + NZ, NZ), core)

    other_core = device(x, y, z, 1 - core)

    def remote(src, dst, send, recv, where):
        return pltpu.make_async_remote_copy(
            src_ref=src, dst_ref=dst, send_sem=send, recv_sem=recv,
            device_id=where, device_id_type=MESH,
        )

    a_copy = pltpu.make_async_copy(a_hbm, a_vmem, a_sem)
    a_copy.start()

    barrier = pltpu.get_barrier_semaphore()
    greeted = [at_x(1), at_x(-1), at_y(1), at_y(-1), at_z(1), at_z(-1), at_z(5), at_z(-5), other_core]
    for where in greeted:
        pl.semaphore_signal(barrier, inc=1, device_id=where, device_id_type=MESH)
    pl.semaphore_wait(barrier, len(greeted))

    sends = []

    def send(src, dst, send_index, recv_index, where):
        copy = remote(src, dst, g_send.at[send_index], g_recv.at[recv_index], where)
        copy.start()
        sends.append(copy)

    def wait_block(recv_index):
        remote(b_ref, relay, g_send.at[0], g_recv.at[recv_index], other_core).wait_recv()

    def x_of(step):
        return lax.rem(x + step + NX, NX)

    def spread(block, half_zhi, half):
        mine = gathered.at[place(half_zhi, x, core)]
        send(block, mine, 2 + 4 * half, 2 + 3 * half, at_x(sign))
        send(block, mine, 3 + 4 * half, 3 + 3 * half, at_x(-sign))
        send(block, mine, 10 + 4 * half, 8 + 4 * half, other_core)

    def collect(half_zhi, half):
        behind = gathered.at[place(half_zhi, x_of(-sign), core)]
        wait_block(2 + 3 * half)
        send(behind, behind, 4 + 4 * half, 4 + 3 * half, at_x(sign))
        send(behind, behind, 11 + 4 * half, 9 + 4 * half, other_core)
        ahead = gathered.at[place(half_zhi, x_of(sign), core)]
        wait_block(3 + 3 * half)
        send(ahead, ahead, 12 + 4 * half, 10 + 4 * half, other_core)

    def collect_far(half_zhi, half):
        far = gathered.at[place(half_zhi, x_of(2), core)]
        wait_block(4 + 3 * half)
        send(far, far, 13 + 4 * half, 11 + 4 * half, other_core)

    send(b_ref, relay, 0, 0, at_z(5 * sign))
    spread(b_ref, zhi, 0)
    gathered[row] = b_ref[...]

    a_copy.wait()

    @pl.loop(0, NL)
    def _(k):
        hi, lo = split_hi_lo(a_vmem[k])
        a_hi[k] = hi
        a_lo[k] = lo

    collect(zhi, 0)
    wait_block(0)
    next_zhi = lax.div(lax.rem(z + sign + NZ, NZ), NL)
    send(relay, gathered.at[place(1 - next_zhi, x, core)], 1, 1, at_z(sign))
    collect_far(zhi, 0)
    wait_block(1)
    spread(gathered.at[place(1 - zhi, x, core)], 1 - zhi, 1)
    collect(1 - zhi, 1)
    collect_far(1 - zhi, 1)
    for k in range(8):
        wait_block(8 + k)

    @pl.loop(0, 8)
    def _(k):
        value = gathered[pl.ds(2 * k, 2)].reshape(2 * WIN, DEPTH)
        hi, lo = split_hi_lo(value)
        rows = pl.ds(pl.multiple_of(2 * WIN * k, 2 * WIN), 2 * WIN)
        b_hi[rows] = hi
        b_lo[rows] = lo

    def product(hi, lo, first):
        bh, bl = b_hi[first : first + CW], b_lo[first : first + CW]

        def dot(p, q):
            return lax.dot_general(
                p, q, (((1,), (1,)), ((), ())), preferred_element_type=jnp.float32
            )

        return dot(hi, bh) + (dot(hi, bl) + dot(lo, bh))

    def y_product(direction, dest):
        hi = a_hi[:, dest].reshape(NL * RB, DEPTH)
        lo = a_lo[:, dest].reshape(NL * RB, DEPTH)
        return product(hi, lo, direction * CW).reshape(NL, RB, CW)

    def z_product(dest):
        hi = a_hi[dest].reshape(NY * RB, DEPTH)
        lo = a_lo[dest].reshape(NY * RB, DEPTH)
        return product(hi, lo, 2 * CW).reshape(NY, RB, CW)

    ypieces = [pl.ds(0, 3), pl.ds(3, 3)]
    zpieces = [pl.ds(0, 4), pl.ds(4, 4)]

    def y_copy(direction, slot, piece):
        part = ypieces[piece]
        return remote(
            ybuf.at[direction, slot, part], ybuf.at[direction, slot + 1, part],
            y_send.at[direction, slot, piece], y_recv.at[direction, slot, piece],
            at_y(1 - 2 * direction),
        )

    def z_copy(way, slot, piece):
        buf = (zup, zdown)[way]
        part = zpieces[piece]
        return remote(
            buf.at[slot, part], buf.at[slot, part],
            z_send.at[way, slot, piece], z_recv.at[way, slot, piece], at_z(1 - 2 * way),
        )

    def z_step(turn):
        for way in range(2):
            far = i if way == 0 else NL - 1 - i
            buf = (zup, zdown)[way]

            @pl.when(turn >= far)
            def _():
                slot = turn - far
                dest = NL - 1 - slot if way == 0 else slot

                @pl.when(far == 0)
                def _():
                    buf[slot] = z_product(dest)
                    for piece in range(2):
                        z_copy(way, slot, piece).start()

                @pl.when(far > 0)
                def _():
                    zpart[...] = z_product(dest)
                    for piece in range(2):
                        z_copy(way, slot, piece).wait_recv()
                        buf[slot, zpieces[piece]] += zpart[zpieces[piece]]
                        z_copy(way, slot, piece).start()

    for direction in range(2):
        dest = lax.rem(y - 1 + 2 * direction + NY, NY)
        ybuf[direction, 0] = y_product(direction, dest)
        for piece in range(2):
            y_copy(direction, 0, piece).start()
    z_step(0)

    @pl.loop(0, NY - 1)
    def _(r):
        for direction in range(2):
            dest = lax.rem(y + (2 + r) * (2 * direction - 1) + 2 * NY, NY)
            ypart[direction] = y_product(direction, dest)
        for piece in range(2):
            for direction in range(2):
                part = ypieces[piece]
                y_copy(direction, r, piece).wait_recv()
                ybuf[direction, r + 1, part] += ypart[direction, part]

                @pl.when(r < NY - 2)
                def _():
                    y_copy(direction, r + 1, piece).start()

        @pl.when((r < 2) | (r == 3) | (r == 4))
        def _():
            z_step(jnp.where(r < 2, r + 1, r))

    usum[...] = z_product(i)
    for way in range(2):
        far = i if way == 0 else NL - 1 - i
        buf = (zup, zdown)[way]

        @pl.when(far > 0)
        def _():
            slot = NL - 1 - far
            for piece in range(2):
                z_copy(way, slot, piece).wait_recv()
                usum[zpieces[piece]] += buf[slot, zpieces[piece]]

    def w_copy(way, slot):
        buf = (wup, wdown)[way]
        return remote(
            buf.at[slot], buf.at[slot], w_send.at[way, slot], w_recv.at[way, slot], at_z(1 - 2 * way)
        )

    def w_step(turn):
        for way in range(2):
            far = i if way == 0 else NL - 1 - i
            buf = (wup, wdown)[way]

            @pl.when(turn >= far)
            def _():
                slot = turn - far
                dest = NL - 1 - slot if way == 0 else slot

                @pl.when(far == 0)
                def _():
                    buf[slot] = ybuf[:, NY - 1, dest]

                @pl.when(far > 0)
                def _():
                    w_copy(way, slot).wait_recv()
                    buf[slot] += ybuf[:, NY - 1, dest]

                w_copy(way, slot).start()

    half = RB // 2

    def u_copy(direction, slot):
        return remote(
            ubuf.at[direction, slot], ubuf.at[direction, slot + 1],
            u_send.at[direction, slot], u_recv.at[direction, slot], at_y(1 - 2 * direction),
        )

    w_step(0)
    for direction in range(2):
        dest = lax.rem(y - 1 + 2 * direction + NY, NY)
        ubuf[direction, 0] = usum[dest, direction * half : (direction + 1) * half]
        u_copy(direction, 0).start()

    @pl.loop(0, NY - 1)
    def _(r):
        for direction in range(2):
            dest = lax.rem(y + (2 + r) * (2 * direction - 1) + 2 * NY, NY)
            u_copy(direction, r).wait_recv()
            ubuf[direction, r + 1] += usum[dest, direction * half : (direction + 1) * half]

            @pl.when(r < NY - 2)
            def _():
                u_copy(direction, r + 1).start()

        @pl.when((r == 1) | (r == 3) | (r == 4) | (r == 6))
        def _():
            w_step(jnp.where(r == 1, 1, jnp.where(r == 3, 2, jnp.where(r == 4, 3, 4))))

    for direction in range(2):
        out_ref[direction * half : (direction + 1) * half, 2 * CW :] = ubuf[direction, NY - 1]
        out_ref[:, direction * CW : (direction + 1) * CW] = ybuf[direction, NY - 1, i]
    for way in range(2):
        far = i if way == 0 else NL - 1 - i
        buf = (wup, wdown)[way]

        @pl.when(far > 0)
        def _():
            slot = NL - 1 - far
            w_copy(way, slot).wait_recv()
            for direction in range(2):
                out_ref[:, direction * CW : (direction + 1) * CW] += buf[slot, direction]

    for copy in sends:
        copy.wait_send()

    @pl.loop(0, NY - 1)
    def _(r):
        for direction in range(2):
            for piece in range(2):
                y_copy(direction, r, piece).wait_send()
            u_copy(direction, r).wait_send()

    @pl.loop(0, NL - 1)
    def _(slot):
        for way in range(2):
            far = i if way == 0 else NL - 1 - i

            @pl.when(slot < NL - 1 - far)
            def _():
                for piece in range(2):
                    z_copy(way, slot, piece).wait_send()
                w_copy(way, slot).wait_send()


def cycle_rows(amplitudes, intermediates):
    f32, bf16 = jnp.float32, jnp.bfloat16
    vmem, dma = pltpu.VMEM, pltpu.SemaphoreType.DMA
    return pl.pallas_call(
        kernel,
        out_shape=jax.ShapeDtypeStruct((RB, NCOL), f32),
        in_specs=[
            pl.BlockSpec(memory_space=pl.ANY),
            pl.BlockSpec(memory_space=pltpu.VMEM),
        ],
        out_specs=pl.BlockSpec(memory_space=pltpu.VMEM),
        scratch_shapes=[
            vmem((NL, NY, RB, DEPTH), f32),
            vmem((NL, NY, RB, DEPTH), bf16),
            vmem((NL, NY, RB, DEPTH), bf16),
            vmem((4 * NX, WIN, DEPTH), f32),
            vmem((WIN, DEPTH), f32),
            vmem((NCOL, DEPTH), bf16),
            vmem((NCOL, DEPTH), bf16),
            vmem((2, NY, NL, RB, CW), f32),
            vmem((2, NL, RB, CW), f32),
            vmem((NL - 1, NY, RB, CW), f32),
            vmem((NL - 1, NY, RB, CW), f32),
            vmem((NY, RB, CW), f32),
            vmem((NL - 1, 2, RB, CW), f32),
            vmem((NL - 1, 2, RB, CW), f32),
            vmem((NY, RB, CW), f32),
            vmem((2, NY, RB // 2, CW), f32),
            dma,
            dma((18,)),
            dma((16,)),
            dma((2, NY - 1, 2)),
            dma((2, NY - 1, 2)),
            dma((2, NL - 1, 2)),
            dma((2, NL - 1, 2)),
            dma((2, NL - 1)),
            dma((2, NL - 1)),
            dma((2, NY - 1)),
            dma((2, NY - 1)),
        ],
        compiler_params=pltpu.CompilerParams(
            collective_id=0, has_side_effects=True, vmem_limit_bytes=60 * 2**20
        ),
    )(amplitudes.reshape(NL, NY, RB, DEPTH), intermediates)


def on_device(
    amplitudes,
    intermediates,
    integrals,
    row_pairs,
    window_virtuals,
    occupied_energies,
    virtual_energies,
):
    cycle_term = cycle_rows(amplitudes, intermediates)
    gap_row = lookup_table(row_pairs[0], virtual_energies) - lookup_table(
        row_pairs[1], occupied_energies
    )
    window_energy = lookup_table(window_virtuals, virtual_energies)
    gap_col = (window_energy[:, None] - occupied_energies[None, :]).reshape(-1)
    return (integrals + cycle_term) / (gap_row[:, None] + gap_col[None, :])


def solution(mesh):
    in_specs = (
        P("row", "col"),
        P("row", "col"),
        P(("row", "col"), None),
        P(None, ("row", "col")),
        P(),
        P(),
        P(),
    )
    out_specs = P(("row", "col"), None)
    return jax.shard_map(
        on_device, mesh=mesh, in_specs=in_specs, out_specs=out_specs, check_vma=False
    )
```

```python
import jax
import jax.numpy as jnp
from jax import lax
from jax.experimental import pallas as pl
from jax.experimental.pallas import tpu as pltpu
from jax.sharding import PartitionSpec as P

MESH = pl.DeviceIdType.MESH
NX, NY, NZ, NL = 4, 8, 12, 6
RB = 32
DEPTH = 512
WIN = 72
HALF = 576
NCOL, NV, NO, NB = 1152, 384, 64, 18

Y_STREAMS = ((0, 256), (512, 512))
Z_STREAMS = ((256, 256), (1024, 128))
Y_PIECES = (3, 3)


def split_hi_lo(value):
    hi = value.astype(jnp.bfloat16)
    return hi, (value - hi.astype(jnp.float32)).astype(jnp.bfloat16)


def as_column(line):
    n = line.shape[1]
    here = lax.broadcasted_iota(jnp.int32, (n, n), 0) == lax.broadcasted_iota(jnp.int32, (n, n), 1)
    return jnp.sum(jnp.where(here, jnp.broadcast_to(line, (n, n)), jnp.zeros_like(line)), axis=1, keepdims=True)


def look_up(indices, table):
    n, m = indices.shape[0], table.shape[1]
    match = indices == lax.broadcasted_iota(jnp.int32, (n, m), 1)
    return jnp.sum(jnp.where(match, jnp.broadcast_to(table, (n, m)), 0.0), axis=1, keepdims=True)


def kernel(
    a_hbm, b_ref, integrals_hbm, pairs_ref, window_ref, occupied_ref, virtual_ref, out_ref,
    a_vmem, integrals, a_hi, a_lo, gathered, b_hi, b_lo, result,
    yc0, yc1, yb0, yb1, zc0, zc1, zup0, zup1, zdn0, zdn1,
    wup0, wup1, wdn0, wdn1, ub0, ub1,
    l_sem, g_send, g_recv, y_send0, y_recv0, y_send1, y_recv1, z_send, z_recv, w_send, w_recv, u_send, u_recv,
):
    ycs, ybs, y_sends, y_recvs = (yc0, yc1), (yb0, yb1), (y_send0, y_send1), (y_recv0, y_recv1)
    zcs, zbufs = (zc0, zc1), ((zup0, zdn0), (zup1, zdn1))
    wbufs, ubs = ((wup0, wdn0), (wup1, wdn1)), (ub0, ub1)

    row, col = lax.axis_index("row"), lax.axis_index("col")
    core = lax.rem(row, 2)
    x = lax.rem(lax.div(row, 2), NX)
    zhi = lax.div(row, 2 * NX)
    y = lax.rem(col, NY)
    i = lax.div(col, NY)
    z = zhi * NL + i
    sign = 1 - 2 * core

    def device(x_, y_, z_, core_):
        return {
            "row": (lax.div(z_, NL) * NX + x_) * 2 + core_,
            "col": lax.rem(z_, NL) * NY + y_,
        }

    def x_of(step):
        return lax.rem(x + step + NX, NX)

    def at_x(step):
        return device(x_of(step), y, z, core)

    def at_y(step):
        return device(x, lax.rem(y + step + NY, NY), z, core)

    def at_z(step):
        return device(x, y, lax.rem(z + step + NZ, NZ), core)

    other_core = device(x, y, z, 1 - core)

    def remote(src, dst, send, recv, where):
        return pltpu.make_async_remote_copy(
            src_ref=src, dst_ref=dst, send_sem=send, recv_sem=recv,
            device_id=where, device_id_type=MESH,
        )

    a_copy = pltpu.make_async_copy(a_hbm, a_vmem, l_sem.at[0])
    a_copy.start()
    i_copy = pltpu.make_async_copy(integrals_hbm, integrals, l_sem.at[1])
    i_copy.start()

    barrier = pltpu.get_barrier_semaphore()
    greeted = [at_x(1), at_x(-1), at_z(1), at_z(-1), at_z(6), other_core]
    greeted += [at_y(k) for k in range(1, NY)]
    for where in greeted:
        pl.semaphore_signal(barrier, inc=1, device_id=where, device_id_type=MESH)
    pl.semaphore_wait(barrier, len(greeted))

    events = []
    finish = []

    def event(when, do):
        events.append((when, len(events), do))

    def slot(half, x_, core_):
        return gathered.at[half, x_ * 2 + core_]

    def send(src, dst, send_index, recv_index, where):
        copy = remote(src, dst, g_send.at[send_index], g_recv.at[recv_index], where)
        copy.start()
        finish.append(copy.wait_send)

    def wait_block(recv_index):
        remote(b_ref, slot(0, x, core), g_send.at[0], g_recv.at[recv_index], other_core).wait_recv()

    def spread(block, half):
        mine = slot(half, x, core)
        send(block, mine, 1 + 7 * half, 1 + 7 * half, at_x(sign))
        send(block, mine, 2 + 7 * half, 2 + 7 * half, at_x(-sign))
        send(block, mine, 3 + 7 * half, 3 + 7 * half, other_core)

    def collect(half):
        behind = slot(half, x_of(-sign), core)
        wait_block(1 + 7 * half)
        send(behind, behind, 4 + 7 * half, 4 + 7 * half, at_x(sign))
        send(behind, behind, 5 + 7 * half, 5 + 7 * half, other_core)
        ahead = slot(half, x_of(sign), core)
        wait_block(2 + 7 * half)
        send(ahead, ahead, 6 + 7 * half, 6 + 7 * half, other_core)

    def collect_far(half):
        far = slot(half, x_of(2), core)
        wait_block(4 + 7 * half)
        send(far, far, 7 + 7 * half, 7 + 7 * half, other_core)

    def split_b(half):
        for k in (3, 5, 6, 7):
            wait_block(k + 7 * half)

        @pl.loop(0, 4)
        def _(k):
            hi, lo = split_hi_lo(gathered[half, pl.ds(2 * k, 2)].reshape(2 * WIN, DEPTH))
            rows = pl.ds(pl.multiple_of(HALF * half + 2 * WIN * k, 2 * WIN), 2 * WIN)
            b_hi[rows] = hi
            b_lo[rows] = lo

    def multiply(target, first, width):
        bh, bl = b_hi[first : first + width], b_lo[first : first + width]

        def dot(p, q):
            return lax.dot_general(
                p, q, (((1,), (1,)), ((), ())), preferred_element_type=jnp.float32
            )

        @pl.loop(0, NL)
        def _(k):
            hi = a_hi[k].reshape(NY * RB, DEPTH)
            lo = a_lo[k].reshape(NY * RB, DEPTH)
            value = dot(hi, bh) + (dot(hi, bl) + dot(lo, bh))
            target[k] = value.reshape(NY, RB, width)

    def y_rows(n, direction, piece):
        size = 3 // Y_PIECES[n]
        return pl.ds(3 * direction + piece * size, size)

    def y_dest(direction, step):
        return lax.rem(y + (1 + step) * (2 * direction - 1) + NY, NY)

    def y_copy(n, direction, step, piece):
        rows = y_rows(n, direction, piece)
        src = ycs[n].at[rows, y_dest(direction, 0)] if step == 0 else ybs[n].at[step - 1, rows]
        index = (direction, step, piece)
        return remote(
            src, ybs[n].at[step, rows], y_sends[n].at[index], y_recvs[n].at[index],
            at_y(1 - 2 * direction),
        )

    def y_start(n, piece):
        for direction in range(2):
            y_copy(n, direction, 0, piece).start()

    def y_step(n, step, piece):
        for direction in range(2):
            rows = y_rows(n, direction, piece)
            y_copy(n, direction, step, piece).wait_recv()
            ybs[n][step, rows] += ycs[n][rows, y_dest(direction, step + 1)]
            if step < NY - 2:
                y_copy(n, direction, step + 1, piece).start()

    def line(bufs, own, parts, sends, recvs, n):
        def copy(way, index, piece, src):
            part = parts[piece]
            return remote(
                src, bufs[way].at[index, part],
                sends.at[n, way, index, piece], recvs.at[n, way, index, piece], at_z(1 - 2 * way),
            )

        def turn(count):
            for way in range(2):
                far = i if way == 0 else NL - 1 - i
                index = count - far
                dest = NL - 1 - index if way == 0 else index

                @pl.when(far == 0)
                def _():
                    for piece in range(2):
                        copy(way, index, piece, own.at[dest, parts[piece]]).start()

                @pl.when((far > 0) & (far <= count))
                def _():
                    for piece in range(2):
                        part = parts[piece]
                        held = bufs[way].at[index, part]
                        copy(way, index, piece, held).wait_recv()
                        bufs[way][index, part] += own[dest, part]
                        copy(way, index, piece, held).start()

        def last():
            for way in range(2):
                far = i if way == 0 else NL - 1 - i
                index = NL - 1 - far

                @pl.when(far > 0)
                def _():
                    for piece in range(2):
                        part = parts[piece]
                        copy(way, index, piece, bufs[way].at[index, part]).wait_recv()
                        own[i, part] += bufs[way][index, part]

        def sent():
            for way in range(2):
                far = i if way == 0 else NL - 1 - i

                @pl.loop(0, NL - 1)
                def _(index):
                    @pl.when(index < NL - 1 - far)
                    def _():
                        for piece in range(2):
                            copy(way, index, piece, bufs[way].at[index, parts[piece]]).wait_send()

        finish.append(sent)
        return turn, last

    half_rows = [pl.ds(0, RB // 2), pl.ds(RB // 2, RB // 2)]
    half_y = [pl.ds(0, NY // 2), pl.ds(NY // 2, NY // 2)]
    z_lines = [line(zbufs[n], zcs[n], half_y, z_send, z_recv, n) for n in range(2)]
    w_lines = [line(wbufs[n], ybs[n].at[NY - 2], half_rows, w_send, w_recv, n) for n in range(2)]

    def u_copy(n, k):
        return remote(
            zcs[n].at[i, lax.rem(y + k, NY)], ubs[n].at[k - 1],
            u_send.at[n, k - 1], u_recv.at[n, k - 1], at_y(k),
        )

    def u_start(n):
        for k in (4, 3, 5, 2, 6, 1, 7):
            u_copy(n, k).start()

    def u_last(n):
        first, width = Z_STREAMS[n]
        total = zcs[n][i, y]
        for k in range(1, NY):
            u_copy(n, k).wait_recv()
            total = total + ubs[n][k - 1]
        result[:, first : first + width] = total

    def w_last(n):
        first, width = Y_STREAMS[n]
        w_lines[n][1]()
        result[:, first : first + width] = ybs[n][NY - 2, i]

    send(b_ref, slot(1, x, core), 0, 0, at_z(6))
    spread(b_ref, 0)
    gathered[0, x * 2 + core] = b_ref[...]
    a_copy.wait()

    @pl.loop(0, NL)
    def _(k):
        hi, lo = split_hi_lo(a_vmem[k])
        a_hi[k] = hi
        a_lo[k] = lo

    event(5.0, lambda: collect(0))
    event(8.5, lambda: collect_far(0))
    event(10.5, lambda: split_b(0))
    event(11.0, lambda: multiply(ycs[0], *Y_STREAMS[0]))
    for piece in range(Y_PIECES[0]):
        event(12.5, lambda piece=piece: y_start(0, piece))
    event(13.0, lambda: multiply(zcs[0], *Z_STREAMS[0]))
    event(14.0, lambda: z_lines[0][0](0))

    def pair():
        wait_block(0)
        spread(slot(1, x, core), 1)

    event(15.0, pair)
    event(20.0, lambda: collect(1))
    event(23.5, lambda: collect_far(1))
    event(26.0, lambda: split_b(1))
    event(26.5, lambda: multiply(ycs[1], *Y_STREAMS[1]))
    for piece in range(Y_PIECES[1]):
        event(30.0, lambda piece=piece: y_start(1, piece))
    event(30.2, lambda: multiply(zcs[1], *Z_STREAMS[1]))
    event(31.0, lambda: z_lines[1][0](0))
    for n, begin, period in ((0, 13.0, 2.6), (1, 30.0, 4.3)):
        for step in range(NY - 1):
            for piece in range(Y_PIECES[n]):
                when = begin + period * (step + (piece + 1) / Y_PIECES[n])
                event(when, lambda n=n, step=step, piece=piece: y_step(n, step, piece))
    for lines, n, begin, period in (
        (z_lines, 0, 15.0, 6.5), (z_lines, 1, 31.0, 6.5), (w_lines, 0, 32.0, 5.0), (w_lines, 1, 60.5, 2.6),
    ):
        for count in range(0 if lines is w_lines else 1, NL - 1):
            event(begin + period * count, lambda lines=lines, n=n, count=count: lines[n][0](count))
    event(47.5, z_lines[0][1])
    event(47.6, lambda: u_start(0))
    event(57.0, lambda: w_last(0))
    event(63.9, z_lines[1][1])
    event(64.0, lambda: u_start(1))
    event(72.0, lambda: u_last(0))
    event(72.1, lambda: u_last(1))
    event(73.5, lambda: w_last(1))
    for _, _, do in sorted(events, key=lambda e: e[:2]):
        do()

    i_copy.wait()
    pairs = pairs_ref[...]
    gap_row = look_up(as_column(pairs[0:1]), virtual_ref[...]) - look_up(as_column(pairs[1:2]), occupied_ref[...])
    energy = look_up(as_column(window_ref[...]), virtual_ref[...])
    block = lax.broadcasted_iota(jnp.int32, (NB, NCOL), 1) // NO == lax.broadcasted_iota(jnp.int32, (NB, NCOL), 0)
    energy = jnp.sum(jnp.where(block, jnp.broadcast_to(energy, (NB, NCOL)), 0.0), axis=0, keepdims=True)
    within = lax.broadcasted_iota(jnp.int32, (NO, NCOL), 1) % NO == lax.broadcasted_iota(jnp.int32, (NO, NCOL), 0)
    occupied = jnp.broadcast_to(as_column(occupied_ref[...]), (NO, NCOL))
    gap_col = energy - jnp.sum(jnp.where(within, occupied, 0.0), axis=0, keepdims=True)
    value = result[...]
    turned = jnp.concatenate([value[:, HALF:], value[:, :HALF]], axis=1)
    cycle_term = jnp.where(zhi == 0, value, turned)
    out_ref[...] = (integrals[...] + cycle_term) / (gap_row + gap_col)

    for wait in finish:
        wait()
    for n in range(2):
        for direction in range(2):
            for step in range(NY - 1):
                for piece in range(Y_PIECES[n]):
                    y_copy(n, direction, step, piece).wait_send()
        for k in range(1, NY):
            u_copy(n, k).wait_send()


def on_device(
    amplitudes, intermediates, integrals, row_pairs, window_virtuals, occupied_energies, virtual_energies
):
    f32, bf16 = jnp.float32, jnp.bfloat16
    vmem, dma = pltpu.VMEM, pltpu.SemaphoreType.DMA
    y_widths, z_widths = [w for _, w in Y_STREAMS], [w for _, w in Z_STREAMS]
    whole, away = pl.BlockSpec(memory_space=pltpu.VMEM), pl.BlockSpec(memory_space=pl.ANY)
    return pl.pallas_call(
        kernel,
        out_shape=jax.ShapeDtypeStruct((RB, NCOL), f32),
        in_specs=[away, whole, away, whole, whole, whole, whole],
        out_specs=whole,
        scratch_shapes=[
            vmem((NL, NY, RB, DEPTH), f32),
            vmem((RB, NCOL), f32),
            vmem((NL, NY, RB, DEPTH), bf16),
            vmem((NL, NY, RB, DEPTH), bf16),
            vmem((2, 2 * NX, WIN, DEPTH), f32),
            vmem((NCOL, DEPTH), bf16),
            vmem((NCOL, DEPTH), bf16),
            vmem((RB, NCOL), f32),
            *[vmem((NL, NY, RB, w), f32) for w in y_widths],
            *[vmem((NY - 1, NL, RB, w), f32) for w in y_widths],
            *[vmem((NL, NY, RB, w), f32) for w in z_widths],
            *[vmem((NL - 1, NY, RB, w), f32) for w in z_widths],
            *[vmem((NL - 1, NY, RB, w), f32) for w in z_widths],
            *[vmem((NL - 1, RB, w), f32) for w in y_widths],
            *[vmem((NL - 1, RB, w), f32) for w in y_widths],
            *[vmem((NY - 1, RB, w), f32) for w in z_widths],
            dma((2,)),
            dma((15,)),
            dma((15,)),
            dma((2, NY - 1, Y_PIECES[0])),
            dma((2, NY - 1, Y_PIECES[0])),
            dma((2, NY - 1, Y_PIECES[1])),
            dma((2, NY - 1, Y_PIECES[1])),
            dma((2, 2, NL - 1, 2)),
            dma((2, 2, NL - 1, 2)),
            dma((2, 2, NL - 1, 2)),
            dma((2, 2, NL - 1, 2)),
            dma((2, NY - 1)),
            dma((2, NY - 1)),
        ],
        compiler_params=pltpu.CompilerParams(
            collective_id=0, has_side_effects=True, vmem_limit_bytes=60 * 2**20
        ),
    )(
        amplitudes.reshape(NL, NY, RB, DEPTH), intermediates, integrals, row_pairs,
        window_virtuals.reshape(1, NB), occupied_energies.reshape(1, NO), virtual_energies.reshape(1, NV),
    )


def solution(mesh):
    in_specs = (
        P("row", "col"),
        P("row", "col"),
        P(("row", "col"), None),
        P(None, ("row", "col")),
        P(),
        P(),
        P(),
    )
    out_specs = P(("row", "col"), None)
    return jax.shard_map(
        on_device, mesh=mesh, in_specs=in_specs, out_specs=out_specs, check_vma=False
    )
```

```python
import jax
import jax.numpy as jnp
from jax import lax
from jax.experimental import pallas as pl
from jax.experimental.pallas import tpu as pltpu
from jax.sharding import PartitionSpec as P

MESH = pl.DeviceIdType.MESH
NX, NY, NZ, NL = 4, 8, 12, 6
RB = 32
DEPTH = 512
WIN = 72
HALF = 576
NCOL, NV, NO, NB = 1152, 384, 64, 18

Y_STREAMS = ((0, 384), (512, 256), (768, 128))
Z_STREAMS = ((384, 128), (896, 256))
Y_PIECES = (3, 3, 1)


def split_hi_lo(value):
    hi = value.astype(jnp.bfloat16)
    return hi, (value - hi.astype(jnp.float32)).astype(jnp.bfloat16)


def as_column(line):
    n = line.shape[1]
    here = lax.broadcasted_iota(jnp.int32, (n, n), 0) == lax.broadcasted_iota(jnp.int32, (n, n), 1)
    return jnp.sum(jnp.where(here, jnp.broadcast_to(line, (n, n)), jnp.zeros_like(line)), axis=1, keepdims=True)


def look_up(indices, table):
    n, m = indices.shape[0], table.shape[1]
    match = indices == lax.broadcasted_iota(jnp.int32, (n, m), 1)
    return jnp.sum(jnp.where(match, jnp.broadcast_to(table, (n, m)), 0.0), axis=1, keepdims=True)


def kernel(
    a_hbm, b_ref, integrals_hbm, pairs_ref, window_ref, occupied_ref, virtual_ref, out_ref,
    a_vmem, integrals, a_hi, a_lo, gathered, b_hi, b_lo, result, gaps,
    yc0, yc1, yc2, yb0, yb1, yb2, zc0, zc1, zup0, zup1, zdn0, zdn1, wb0, wb1, wb2, ub0, ub1,
    l_sem, g_send, g_recv, ys0, yr0, ys1, yr1, ys2, yr2, z_send, z_recv, w_send, w_recv, u_send, u_recv,
):
    ycs, ybs, wbs = (yc0, yc1, yc2), (yb0, yb1, yb2), (wb0, wb1, wb2)
    y_sends, y_recvs = (ys0, ys1, ys2), (yr0, yr1, yr2)
    zcs, zbufs, ubs = (zc0, zc1), ((zup0, zdn0), (zup1, zdn1)), (ub0, ub1)

    row, col = lax.axis_index("row"), lax.axis_index("col")
    core = lax.rem(row, 2)
    x = lax.rem(lax.div(row, 2), NX)
    zhi = lax.div(row, 2 * NX)
    y = lax.rem(col, NY)
    i = lax.div(col, NY)
    z = zhi * NL + i
    sign = 1 - 2 * core

    def device(x_, y_, z_, core_):
        return {
            "row": (lax.div(z_, NL) * NX + x_) * 2 + core_,
            "col": lax.rem(z_, NL) * NY + y_,
        }

    def x_of(step):
        return lax.rem(x + step + NX, NX)

    def at_x(step):
        return device(x_of(step), y, z, core)

    def at_y(step):
        return device(x, lax.rem(y + step + NY, NY), z, core)

    def at_z(step):
        return device(x, y, lax.rem(z + step + NZ, NZ), core)

    def in_run(dest):
        return device(x, y, zhi * NL + dest, core)

    other_core = device(x, y, z, 1 - core)

    def remote(src, dst, send, recv, where):
        return pltpu.make_async_remote_copy(
            src_ref=src, dst_ref=dst, send_sem=send, recv_sem=recv,
            device_id=where, device_id_type=MESH,
        )

    a_copy = pltpu.make_async_copy(a_hbm, a_vmem, l_sem.at[0])
    a_copy.start()
    i_copy = pltpu.make_async_copy(integrals_hbm, integrals, l_sem.at[1])
    i_copy.start()

    barrier = pltpu.get_barrier_semaphore()
    greeted = [at_z(6), at_x(1), at_x(-1), other_core]
    greeted += [at_y(k) for k in range(1, NY)]
    for dest in range(NL):
        @pl.when(dest != i)
        def _():
            pl.semaphore_signal(barrier, inc=1, device_id=in_run(dest), device_id_type=MESH)

    for where in greeted:
        pl.semaphore_signal(barrier, inc=1, device_id=where, device_id_type=MESH)
    pl.semaphore_wait(barrier, len(greeted) + NL - 1)

    events = []
    finish = []

    def event(when, do):
        events.append((when, len(events), do))

    def slot(half, x_, core_):
        return gathered.at[half, x_ * 2 + core_]

    def send(src, dst, send_index, recv_index, where):
        copy = remote(src, dst, g_send.at[send_index], g_recv.at[recv_index], where)
        copy.start()
        finish.append(copy.wait_send)

    def wait_block(recv_index):
        remote(b_ref, slot(0, x, core), g_send.at[0], g_recv.at[recv_index], other_core).wait_recv()

    def spread(block, half):
        mine = slot(half, x, core)
        send(block, mine, 1 + 7 * half, 1 + 7 * half, at_x(sign))
        send(block, mine, 2 + 7 * half, 2 + 7 * half, at_x(-sign))
        send(block, mine, 3 + 7 * half, 3 + 7 * half, other_core)

    def collect(half):
        behind = slot(half, x_of(-sign), core)
        wait_block(1 + 7 * half)
        send(behind, behind, 4 + 7 * half, 4 + 7 * half, at_x(sign))
        send(behind, behind, 5 + 7 * half, 5 + 7 * half, other_core)
        ahead = slot(half, x_of(sign), core)
        wait_block(2 + 7 * half)
        send(ahead, ahead, 6 + 7 * half, 6 + 7 * half, other_core)

    def collect_far(half):
        far = slot(half, x_of(2), core)
        wait_block(4 + 7 * half)
        send(far, far, 7 + 7 * half, 7 + 7 * half, other_core)

    def split_b(half):
        for k in (3, 5, 6, 7):
            wait_block(k + 7 * half)

        @pl.loop(0, 4)
        def _(k):
            hi, lo = split_hi_lo(gathered[half, pl.ds(2 * k, 2)].reshape(2 * WIN, DEPTH))
            rows = pl.ds(pl.multiple_of(HALF * half + 2 * WIN * k, 2 * WIN), 2 * WIN)
            b_hi[rows] = hi
            b_lo[rows] = lo

    def multiply(target, first, width, k):
        bh, bl = b_hi[first : first + width], b_lo[first : first + width]

        def dot(p, q):
            return lax.dot_general(
                p, q, (((1,), (1,)), ((), ())), preferred_element_type=jnp.float32
            )

        hi = a_hi[k].reshape(NY * RB, DEPTH)
        lo = a_lo[k].reshape(NY * RB, DEPTH)
        value = dot(hi, bh) + (dot(hi, bl) + dot(lo, bh))
        target[k] = value.reshape(NY, RB, width)

    def y_rows(n, direction, piece):
        size = 3 // Y_PIECES[n]
        return pl.ds(3 * direction + piece * size, size)

    def y_dest(direction, step):
        return lax.rem(y + (1 + step) * (2 * direction - 1) + NY, NY)

    def y_copy(n, direction, step, piece):
        rows = y_rows(n, direction, piece)
        src = ycs[n].at[rows, y_dest(direction, 0)] if step == 0 else ybs[n].at[step - 1, rows]
        index = (direction, step, piece)
        return remote(
            src, ybs[n].at[step, rows], y_sends[n].at[index], y_recvs[n].at[index],
            at_y(1 - 2 * direction),
        )

    def y_start(n, direction, piece):
        y_copy(n, direction, 0, piece).start()

    def y_step(n, step, piece):
        for direction in range(2):
            rows = y_rows(n, direction, piece)
            y_copy(n, direction, step, piece).wait_recv()
            ybs[n][step, rows] += ycs[n][rows, y_dest(direction, step + 1)]
            if step < NY - 2:
                y_copy(n, direction, step + 1, piece).start()

    def line(bufs, own, parts, sends, recvs, n):
        def copy(way, index, piece, src):
            part = parts[piece]
            return remote(
                src, bufs[way].at[index, part],
                sends.at[n, way, index, piece], recvs.at[n, way, index, piece], at_z(1 - 2 * way),
            )

        def turn(count):
            for way in range(2):
                far = i if way == 0 else NL - 1 - i
                index = count - far
                dest = NL - 1 - index if way == 0 else index

                @pl.when(far == 0)
                def _():
                    for piece in range(2):
                        copy(way, index, piece, own.at[dest, parts[piece]]).start()

                @pl.when((far > 0) & (far <= count))
                def _():
                    for piece in range(2):
                        part = parts[piece]
                        held = bufs[way].at[index, part]
                        copy(way, index, piece, held).wait_recv()
                        bufs[way][index, part] += own[dest, part]
                        copy(way, index, piece, held).start()

        def last():
            for way in range(2):
                far = i if way == 0 else NL - 1 - i
                index = NL - 1 - far

                @pl.when(far > 0)
                def _():
                    for piece in range(2):
                        part = parts[piece]
                        copy(way, index, piece, bufs[way].at[index, part]).wait_recv()
                        own[i, part] += bufs[way][index, part]

        def sent():
            for way in range(2):
                far = i if way == 0 else NL - 1 - i

                @pl.loop(0, NL - 1)
                def _(index):
                    @pl.when(index < NL - 1 - far)
                    def _():
                        for piece in range(2):
                            copy(way, index, piece, bufs[way].at[index, parts[piece]]).wait_send()

        finish.append(sent)
        return turn, last

    half_y = [pl.ds(0, NY // 2), pl.ds(NY // 2, NY // 2)]
    z_lines = [line(zbufs[n], zcs[n], half_y, z_send, z_recv, n) for n in range(2)]

    def w_copy(n, dest, source):
        return remote(
            ybs[n].at[NY - 2, dest], wbs[n].at[source],
            w_send.at[n, dest], w_recv.at[n, source], in_run(dest),
        )

    def w_start(n):
        for dest in range(NL):
            @pl.when(dest != i)
            def _():
                w_copy(n, dest, i).start()

    def w_last(n):
        first, width = Y_STREAMS[n]
        for source in range(NL):
            @pl.when(source != i)
            def _():
                w_copy(n, i, source).wait_recv()
                ybs[n][NY - 2, i] += wbs[n][source]

        result[:, first : first + width] = ybs[n][NY - 2, i]

    def w_sent(n):
        for dest in range(NL):
            @pl.when(dest != i)
            def _():
                w_copy(n, dest, i).wait_send()

    def u_copy(n, k):
        return remote(
            zcs[n].at[i, lax.rem(y + k, NY)], ubs[n].at[k - 1],
            u_send.at[n, k - 1], u_recv.at[n, k - 1], at_y(k),
        )

    def u_start(n):
        for k in (4, 3, 5, 2, 6, 1, 7):
            u_copy(n, k).start()

    def u_last(n):
        first, width = Z_STREAMS[n]
        total = zcs[n][i, y]
        for k in range(1, NY):
            u_copy(n, k).wait_recv()
            total = total + ubs[n][k - 1]
        result[:, first : first + width] = total

    def find_gaps():
        pairs, window = pairs_ref[...], window_ref[...].reshape(1, NB)
        occupied, virtual = occupied_ref[...].reshape(1, NO), virtual_ref[...].reshape(1, NV)
        gap_row = look_up(as_column(pairs[0:1]), virtual) - look_up(as_column(pairs[1:2]), occupied)
        energy = look_up(as_column(window), virtual)
        block = lax.broadcasted_iota(jnp.int32, (NB, NCOL), 1) // NO == lax.broadcasted_iota(jnp.int32, (NB, NCOL), 0)
        energy = jnp.sum(jnp.where(block, jnp.broadcast_to(energy, (NB, NCOL)), 0.0), axis=0, keepdims=True)
        within = lax.broadcasted_iota(jnp.int32, (NO, NCOL), 1) % NO == lax.broadcasted_iota(jnp.int32, (NO, NCOL), 0)
        occupied = jnp.broadcast_to(as_column(occupied), (NO, NCOL))
        gap_col = energy - jnp.sum(jnp.where(within, occupied, 0.0), axis=0, keepdims=True)
        gaps[...] = gap_row + gap_col

    send(b_ref, slot(1, x, core), 0, 0, at_z(6))
    spread(b_ref, 0)
    gathered[0, x * 2 + core] = b_ref[...]
    a_copy.wait()

    @pl.loop(0, NL)
    def _(k):
        hi, lo = split_hi_lo(a_vmem[k])
        a_hi[k] = hi
        a_lo[k] = lo

    event(5.0, lambda: collect(0))
    event(8.5, lambda: collect_far(0))
    event(11.0, lambda: split_b(0))

    def pair():
        wait_block(0)
        spread(slot(1, x, core), 1)

    def y_begin(n, when, cost):
        size = 3 // Y_PIECES[n]
        for k in range(3):
            for direction in range(2):
                event(when, lambda k=3 * direction + k: multiply(ycs[n], *Y_STREAMS[n], k))
                if (k + 1) % size == 0:
                    event(when, lambda d=direction, p=k // size: y_start(n, d, p))
                when += cost

    def y_go(n, when, period):
        for step in range(NY - 1):
            for piece in range(Y_PIECES[n]):
                at = when + period * (step + (piece + 1) / Y_PIECES[n])
                event(at, lambda step=step, piece=piece: y_step(n, step, piece))
        event(when + period * (NY - 1) + 0.01, lambda: w_start(n))

    def z_begin(n, when, cost):
        for k in (5, 0, 4, 1, 3, 2):
            event(when, lambda k=k: multiply(zcs[n], *Z_STREAMS[n], k))
            when += cost

    def z_go(n, when, period):
        for count in range(NL - 1):
            event(when + period * count, lambda count=count: z_lines[n][0](count))
        event(when + period * (NL - 1), z_lines[n][1])
        event(when + period * (NL - 1) + 0.01, lambda: u_start(n))

    y_begin(0, 11.5, 0.5)
    event(14.7, pair)
    z_begin(0, 14.8, 0.2)
    z_go(0, 16.0, 4.2)
    y_go(0, 14.5, 3.8)
    event(20.0, lambda: collect(1))
    event(23.5, lambda: collect_far(1))
    event(27.0, lambda: split_b(1))
    y_begin(1, 27.5, 0.4)
    z_begin(1, 30.0, 0.4)
    z_go(1, 32.5, 6.0)
    y_begin(2, 33.0, 0.2)
    y_go(1, 30.0, 4.2)
    y_go(2, 36.0, 3.7)
    event(45.0, find_gaps)
    event(57.0, lambda: u_last(0))
    event(58.0, lambda: w_last(0))
    event(75.0, lambda: w_last(1))
    event(76.0, lambda: w_last(2))
    event(77.0, lambda: u_last(1))
    for _, _, do in sorted(events, key=lambda e: e[:2]):
        do()

    i_copy.wait()
    value = result[...]
    turned = jnp.concatenate([value[:, HALF:], value[:, :HALF]], axis=1)
    cycle_term = jnp.where(zhi == 0, value, turned)
    out_ref[...] = (integrals[...] + cycle_term) / gaps[...]

    for wait in finish:
        wait()
    for n in range(len(Y_STREAMS)):
        for direction in range(2):
            for step in range(NY - 1):
                for piece in range(Y_PIECES[n]):
                    y_copy(n, direction, step, piece).wait_send()
        w_sent(n)
    for n in range(len(Z_STREAMS)):
        for k in range(1, NY):
            u_copy(n, k).wait_send()


def on_device(
    amplitudes, intermediates, integrals, row_pairs, window_virtuals, occupied_energies, virtual_energies
):
    f32, bf16 = jnp.float32, jnp.bfloat16
    vmem, dma = pltpu.VMEM, pltpu.SemaphoreType.DMA
    y_widths, z_widths = [w for _, w in Y_STREAMS], [w for _, w in Z_STREAMS]
    whole, away = pl.BlockSpec(memory_space=pltpu.VMEM), pl.BlockSpec(memory_space=pl.ANY)
    return pl.pallas_call(
        kernel,
        out_shape=jax.ShapeDtypeStruct((RB, NCOL), f32),
        in_specs=[away, whole, away, whole, whole, whole, whole],
        out_specs=whole,
        scratch_shapes=[
            vmem((NL, NY, RB, DEPTH), f32),
            vmem((RB, NCOL), f32),
            vmem((NL, NY, RB, DEPTH), bf16),
            vmem((NL, NY, RB, DEPTH), bf16),
            vmem((2, 2 * NX, WIN, DEPTH), f32),
            vmem((NCOL, DEPTH), bf16),
            vmem((NCOL, DEPTH), bf16),
            vmem((RB, NCOL), f32),
            vmem((RB, NCOL), f32),
            *[vmem((NL, NY, RB, w), f32) for w in y_widths],
            *[vmem((NY - 1, NL, RB, w), f32) for w in y_widths],
            *[vmem((NL, NY, RB, w), f32) for w in z_widths],
            *[vmem((NL - 1, NY, RB, w), f32) for w in z_widths],
            *[vmem((NL - 1, NY, RB, w), f32) for w in z_widths],
            *[vmem((NL, RB, w), f32) for w in y_widths],
            *[vmem((NY - 1, RB, w), f32) for w in z_widths],
            dma((2,)),
            dma((15,)),
            dma((15,)),
            *[dma((2, NY - 1, p)) for p in Y_PIECES for _ in range(2)],
            dma((2, 2, NL - 1, 2)),
            dma((2, 2, NL - 1, 2)),
            dma((3, NL)),
            dma((3, NL)),
            dma((2, NY - 1)),
            dma((2, NY - 1)),
        ],
        compiler_params=pltpu.CompilerParams(
            collective_id=0, has_side_effects=True, vmem_limit_bytes=60 * 2**20
        ),
    )(
        amplitudes.reshape(NL, NY, RB, DEPTH), intermediates, integrals, row_pairs,
        window_virtuals, occupied_energies, virtual_energies,
    )


def solution(mesh):
    in_specs = (
        P("row", "col"),
        P("row", "col"),
        P(("row", "col"), None),
        P(None, ("row", "col")),
        P(),
        P(),
        P(),
    )
    out_specs = P(("row", "col"), None)
    return jax.shard_map(
        on_device, mesh=mesh, in_specs=in_specs, out_specs=out_specs, check_vma=False
    )
```

```python
import jax
import jax.numpy as jnp
from jax import lax
from jax.experimental import pallas as pl
from jax.experimental.pallas import tpu as pltpu
from jax.sharding import PartitionSpec as P

MESH = pl.DeviceIdType.MESH
NX, NY, NZ, NL = 4, 8, 12, 6
RB = 32
DEPTH = 512
WIN = 72
HALF = 576
NCOL, NV, NO, NB = 1152, 384, 64, 18

Y_STREAMS = ((0, 384), (512, 256), (768, 128))
Z_STREAMS = ((384, 128), (896, 256))
Y_PIECES = (3, 3, 1)


def split_hi_lo(value):
    hi = value.astype(jnp.bfloat16)
    return hi, (value - hi.astype(jnp.float32)).astype(jnp.bfloat16)


def as_column(line):
    n = line.shape[1]
    here = lax.broadcasted_iota(jnp.int32, (n, n), 0) == lax.broadcasted_iota(jnp.int32, (n, n), 1)
    return jnp.sum(jnp.where(here, jnp.broadcast_to(line, (n, n)), jnp.zeros_like(line)), axis=1, keepdims=True)


def look_up(indices, table):
    n, m = indices.shape[0], table.shape[1]
    match = indices == lax.broadcasted_iota(jnp.int32, (n, m), 1)
    return jnp.sum(jnp.where(match, jnp.broadcast_to(table, (n, m)), 0.0), axis=1, keepdims=True)


def kernel(
    a_hbm, b_ref, integrals_hbm, pairs_ref, window_ref, occupied_ref, virtual_ref, out_ref,
    a_vmem, integrals, a_hi, a_lo, gathered, b_hi, b_lo, result, gaps,
    yc0, yc1, yc2, yb0, yb1, yb2, zc0, zc1, zup0, zup1, zdn0, zdn1, wb0, wb1, wb2, ub0, ub1,
    l_sem, g_send, g_recv, ys0, yr0, ys1, yr1, ys2, yr2, z_send, z_recv, w_send, w_recv, u_send, u_recv,
):
    ycs, ybs, wbs = (yc0, yc1, yc2), (yb0, yb1, yb2), (wb0, wb1, wb2)
    y_sends, y_recvs = (ys0, ys1, ys2), (yr0, yr1, yr2)
    zcs, zbufs, ubs = (zc0, zc1), ((zup0, zdn0), (zup1, zdn1)), (ub0, ub1)

    row, col = lax.axis_index("row"), lax.axis_index("col")
    core = lax.rem(row, 2)
    x = lax.rem(lax.div(row, 2), NX)
    zhi = lax.div(row, 2 * NX)
    y = lax.rem(col, NY)
    i = lax.div(col, NY)
    z = zhi * NL + i
    sign = 1 - 2 * core

    def device(x_, y_, z_, core_):
        return {
            "row": (lax.div(z_, NL) * NX + x_) * 2 + core_,
            "col": lax.rem(z_, NL) * NY + y_,
        }

    def x_of(step):
        return lax.rem(x + step + NX, NX)

    def at_x(step):
        return device(x_of(step), y, z, core)

    def at_y(step):
        return device(x, lax.rem(y + step + NY, NY), z, core)

    def at_z(step):
        return device(x, y, lax.rem(z + step + NZ, NZ), core)

    def in_run(dest):
        return device(x, y, zhi * NL + dest, core)

    other_core = device(x, y, z, 1 - core)

    def remote(src, dst, send, recv, where):
        return pltpu.make_async_remote_copy(
            src_ref=src, dst_ref=dst, send_sem=send, recv_sem=recv,
            device_id=where, device_id_type=MESH,
        )

    a_copy = pltpu.make_async_copy(a_hbm, a_vmem, l_sem.at[0])
    a_copy.start()
    i_copy = pltpu.make_async_copy(integrals_hbm, integrals, l_sem.at[1])
    i_copy.start()

    barrier = pltpu.get_barrier_semaphore()
    greeted = [at_z(6), at_x(1), at_x(-1), other_core]
    greeted += [at_y(k) for k in range(1, NY)]
    for dest in range(NL):
        @pl.when(dest != i)
        def _():
            pl.semaphore_signal(barrier, inc=1, device_id=in_run(dest), device_id_type=MESH)

    for where in greeted:
        pl.semaphore_signal(barrier, inc=1, device_id=where, device_id_type=MESH)
    pl.semaphore_wait(barrier, len(greeted) + NL - 1)

    events = []
    finish = []

    def event(when, do):
        events.append((when, len(events), do))

    def slot(half, x_, core_):
        return gathered.at[half, x_ * 2 + core_]

    def send(src, dst, send_index, recv_index, where):
        copy = remote(src, dst, g_send.at[send_index], g_recv.at[recv_index], where)
        copy.start()
        finish.append(copy.wait_send)

    def wait_block(recv_index):
        remote(b_ref, slot(0, x, core), g_send.at[0], g_recv.at[recv_index], other_core).wait_recv()

    def spread(block, half):
        mine = slot(half, x, core)
        send(block, mine, 1 + 7 * half, 1 + 7 * half, at_x(sign))
        send(block, mine, 2 + 7 * half, 2 + 7 * half, at_x(-sign))
        send(block, mine, 3 + 7 * half, 3 + 7 * half, other_core)

    def collect(half):
        behind = slot(half, x_of(-sign), core)
        wait_block(1 + 7 * half)
        send(behind, behind, 4 + 7 * half, 4 + 7 * half, at_x(sign))
        send(behind, behind, 5 + 7 * half, 5 + 7 * half, other_core)
        ahead = slot(half, x_of(sign), core)
        wait_block(2 + 7 * half)
        send(ahead, ahead, 6 + 7 * half, 6 + 7 * half, other_core)

    def collect_far(half):
        far = slot(half, x_of(2), core)
        wait_block(4 + 7 * half)
        send(far, far, 7 + 7 * half, 7 + 7 * half, other_core)

    def split_b(half):
        for k in (3, 5, 6, 7):
            wait_block(k + 7 * half)

        @pl.loop(0, 4)
        def _(k):
            hi, lo = split_hi_lo(gathered[half, pl.ds(2 * k, 2)].reshape(2 * WIN, DEPTH))
            rows = pl.ds(pl.multiple_of(HALF * half + 2 * WIN * k, 2 * WIN), 2 * WIN)
            b_hi[rows] = hi
            b_lo[rows] = lo

    def multiply(target, first, width, k):
        bh, bl = b_hi[first : first + width], b_lo[first : first + width]

        def dot(p, q):
            return lax.dot_general(
                p, q, (((1,), (1,)), ((), ())), preferred_element_type=jnp.float32
            )

        hi = a_hi[k].reshape(NY * RB, DEPTH)
        lo = a_lo[k].reshape(NY * RB, DEPTH)
        value = dot(hi, bh) + (dot(hi, bl) + dot(lo, bh))
        target[k] = value.reshape(NY, RB, width)

    def y_rows(n, direction, piece):
        size = 3 // Y_PIECES[n]
        return pl.ds(3 * direction + piece * size, size)

    def y_dest(direction, step):
        return lax.rem(y + (1 + step) * (2 * direction - 1) + NY, NY)

    def y_copy(n, direction, step, piece):
        rows = y_rows(n, direction, piece)
        src = ycs[n].at[rows, y_dest(direction, 0)] if step == 0 else ybs[n].at[step - 1, rows]
        index = (direction, step, piece)
        return remote(
            src, ybs[n].at[step, rows], y_sends[n].at[index], y_recvs[n].at[index],
            at_y(1 - 2 * direction),
        )

    def y_start(n, direction, piece):
        y_copy(n, direction, 0, piece).start()

    def y_step(n, step, piece):
        for direction in range(2):
            rows = y_rows(n, direction, piece)
            y_copy(n, direction, step, piece).wait_recv()
            ybs[n][step, rows] += ycs[n][rows, y_dest(direction, step + 1)]
            if step < NY - 2:
                y_copy(n, direction, step + 1, piece).start()

    def line(bufs, own, parts, sends, recvs, n):
        def copy(way, index, piece, src):
            part = parts[piece]
            return remote(
                src, bufs[way].at[index, part],
                sends.at[n, way, index, piece], recvs.at[n, way, index, piece], at_z(1 - 2 * way),
            )

        def turn(count):
            for way in range(2):
                far = i if way == 0 else NL - 1 - i
                index = count - far
                dest = NL - 1 - index if way == 0 else index

                @pl.when(far == 0)
                def _():
                    for piece in range(2):
                        copy(way, index, piece, own.at[dest, parts[piece]]).start()

                @pl.when((far > 0) & (far <= count))
                def _():
                    for piece in range(2):
                        part = parts[piece]
                        held = bufs[way].at[index, part]
                        copy(way, index, piece, held).wait_recv()
                        bufs[way][index, part] += own[dest, part]
                        copy(way, index, piece, held).start()

        def last():
            for way in range(2):
                far = i if way == 0 else NL - 1 - i
                index = NL - 1 - far

                @pl.when(far > 0)
                def _():
                    for piece in range(2):
                        part = parts[piece]
                        copy(way, index, piece, bufs[way].at[index, part]).wait_recv()
                        own[i, part] += bufs[way][index, part]

        def sent():
            for way in range(2):
                far = i if way == 0 else NL - 1 - i

                @pl.loop(0, NL - 1)
                def _(index):
                    @pl.when(index < NL - 1 - far)
                    def _():
                        for piece in range(2):
                            copy(way, index, piece, bufs[way].at[index, parts[piece]]).wait_send()

        finish.append(sent)
        return turn, last

    half_y = [pl.ds(0, NY // 2), pl.ds(NY // 2, NY // 2)]
    z_lines = [line(zbufs[n], zcs[n], half_y, z_send, z_recv, n) for n in range(2)]

    def w_copy(n, dest, source):
        return remote(
            ybs[n].at[NY - 2, dest], wbs[n].at[source],
            w_send.at[n, dest], w_recv.at[n, source], in_run(dest),
        )

    def w_start(n):
        for dest in range(NL):
            @pl.when(dest != i)
            def _():
                w_copy(n, dest, i).start()

    def w_last(n):
        first, width = Y_STREAMS[n]
        for source in range(NL):
            @pl.when(source != i)
            def _():
                w_copy(n, i, source).wait_recv()
                ybs[n][NY - 2, i] += wbs[n][source]

        result[:, first : first + width] = ybs[n][NY - 2, i]

    def w_sent(n):
        for dest in range(NL):
            @pl.when(dest != i)
            def _():
                w_copy(n, dest, i).wait_send()

    def u_copy(n, k):
        return remote(
            zcs[n].at[i, lax.rem(y + k, NY)], ubs[n].at[k - 1],
            u_send.at[n, k - 1], u_recv.at[n, k - 1], at_y(k),
        )

    def u_start(n):
        for k in (4, 3, 5, 2, 6, 1, 7):
            u_copy(n, k).start()

    def u_last(n):
        first, width = Z_STREAMS[n]
        total = zcs[n][i, y]
        for k in range(1, NY):
            u_copy(n, k).wait_recv()
            total = total + ubs[n][k - 1]
        result[:, first : first + width] = total

    def find_gaps():
        pairs, window = pairs_ref[...], window_ref[...].reshape(1, NB)
        occupied, virtual = occupied_ref[...].reshape(1, NO), virtual_ref[...].reshape(1, NV)
        gap_row = look_up(as_column(pairs[0:1]), virtual) - look_up(as_column(pairs[1:2]), occupied)
        energy = look_up(as_column(window), virtual)
        block = lax.broadcasted_iota(jnp.int32, (NB, NCOL), 1) // NO == lax.broadcasted_iota(jnp.int32, (NB, NCOL), 0)
        energy = jnp.sum(jnp.where(block, jnp.broadcast_to(energy, (NB, NCOL)), 0.0), axis=0, keepdims=True)
        within = lax.broadcasted_iota(jnp.int32, (NO, NCOL), 1) % NO == lax.broadcasted_iota(jnp.int32, (NO, NCOL), 0)
        occupied = jnp.broadcast_to(as_column(occupied), (NO, NCOL))
        gap_col = energy - jnp.sum(jnp.where(within, occupied, 0.0), axis=0, keepdims=True)
        gaps[...] = gap_row + gap_col

    send(b_ref, slot(1, x, core), 0, 0, at_z(6))
    spread(b_ref, 0)
    gathered[0, x * 2 + core] = b_ref[...]
    a_copy.wait()

    @pl.loop(0, NL)
    def _(k):
        hi, lo = split_hi_lo(a_vmem[k])
        a_hi[k] = hi
        a_lo[k] = lo

    event(5.0, lambda: collect(0))
    event(8.5, lambda: collect_far(0))
    event(11.0, lambda: split_b(0))

    def pair():
        wait_block(0)
        spread(slot(1, x, core), 1)

    def y_begin(n, when, cost):
        size = 3 // Y_PIECES[n]
        for k in range(3):
            for direction in range(2):
                event(when, lambda k=3 * direction + k: multiply(ycs[n], *Y_STREAMS[n], k))
                if (k + 1) % size == 0:
                    event(when, lambda d=direction, p=k // size: y_start(n, d, p))
                when += cost

    def y_go(n, when, period):
        for step in range(NY - 1):
            for piece in range(Y_PIECES[n]):
                at = when + period * (step + (piece + 1) / Y_PIECES[n])
                event(at, lambda step=step, piece=piece: y_step(n, step, piece))
        event(when + period * (NY - 1) + 0.01, lambda: w_start(n))

    def z_begin(n, when, cost):
        for k in (5, 0, 4, 1, 3, 2):
            event(when, lambda k=k: multiply(zcs[n], *Z_STREAMS[n], k))
            when += cost

    def z_go(n, when, period):
        for count in range(NL - 1):
            event(when + period * count, lambda count=count: z_lines[n][0](count))
        event(when + period * (NL - 1), z_lines[n][1])
        event(when + period * (NL - 1) + 0.01, lambda: u_start(n))

    y_begin(0, 11.5, 0.5)
    event(11.3, pair)
    z_begin(0, 14.8, 0.2)
    z_go(0, 16.0, 4.2)
    y_go(0, 14.5, 3.8)
    event(20.0, lambda: collect(1))
    event(23.5, lambda: collect_far(1))
    event(27.0, lambda: split_b(1))
    y_begin(1, 27.5, 0.4)
    z_begin(1, 30.0, 0.4)
    z_go(1, 32.5, 6.0)
    y_begin(2, 33.0, 0.2)
    y_go(1, 30.0, 4.2)
    y_go(2, 36.0, 3.7)
    event(45.0, find_gaps)
    event(57.0, lambda: u_last(0))
    event(58.0, lambda: w_last(0))
    event(75.0, lambda: w_last(1))
    event(76.0, lambda: w_last(2))
    event(77.0, lambda: u_last(1))
    for _, _, do in sorted(events, key=lambda e: e[:2]):
        do()

    i_copy.wait()
    value = result[...]
    turned = jnp.concatenate([value[:, HALF:], value[:, :HALF]], axis=1)
    cycle_term = jnp.where(zhi == 0, value, turned)
    out_ref[...] = (integrals[...] + cycle_term) / gaps[...]

    for wait in finish:
        wait()
    for n in range(len(Y_STREAMS)):
        for direction in range(2):
            for step in range(NY - 1):
                for piece in range(Y_PIECES[n]):
                    y_copy(n, direction, step, piece).wait_send()
        w_sent(n)
    for n in range(len(Z_STREAMS)):
        for k in range(1, NY):
            u_copy(n, k).wait_send()


def on_device(
    amplitudes, intermediates, integrals, row_pairs, window_virtuals, occupied_energies, virtual_energies
):
    f32, bf16 = jnp.float32, jnp.bfloat16
    vmem, dma = pltpu.VMEM, pltpu.SemaphoreType.DMA
    y_widths, z_widths = [w for _, w in Y_STREAMS], [w for _, w in Z_STREAMS]
    whole, away = pl.BlockSpec(memory_space=pltpu.VMEM), pl.BlockSpec(memory_space=pl.ANY)
    return pl.pallas_call(
        kernel,
        out_shape=jax.ShapeDtypeStruct((RB, NCOL), f32),
        in_specs=[away, whole, away, whole, whole, whole, whole],
        out_specs=whole,
        scratch_shapes=[
            vmem((NL, NY, RB, DEPTH), f32),
            vmem((RB, NCOL), f32),
            vmem((NL, NY, RB, DEPTH), bf16),
            vmem((NL, NY, RB, DEPTH), bf16),
            vmem((2, 2 * NX, WIN, DEPTH), f32),
            vmem((NCOL, DEPTH), bf16),
            vmem((NCOL, DEPTH), bf16),
            vmem((RB, NCOL), f32),
            vmem((RB, NCOL), f32),
            *[vmem((NL, NY, RB, w), f32) for w in y_widths],
            *[vmem((NY - 1, NL, RB, w), f32) for w in y_widths],
            *[vmem((NL, NY, RB, w), f32) for w in z_widths],
            *[vmem((NL - 1, NY, RB, w), f32) for w in z_widths],
            *[vmem((NL - 1, NY, RB, w), f32) for w in z_widths],
            *[vmem((NL, RB, w), f32) for w in y_widths],
            *[vmem((NY - 1, RB, w), f32) for w in z_widths],
            dma((2,)),
            dma((15,)),
            dma((15,)),
            *[dma((2, NY - 1, p)) for p in Y_PIECES for _ in range(2)],
            dma((2, 2, NL - 1, 2)),
            dma((2, 2, NL - 1, 2)),
            dma((3, NL)),
            dma((3, NL)),
            dma((2, NY - 1)),
            dma((2, NY - 1)),
        ],
        compiler_params=pltpu.CompilerParams(
            collective_id=0, has_side_effects=True, vmem_limit_bytes=60 * 2**20
        ),
    )(
        amplitudes.reshape(NL, NY, RB, DEPTH), intermediates, integrals, row_pairs,
        window_virtuals, occupied_energies, virtual_energies,
    )


def solution(mesh):
    in_specs = (
        P("row", "col"),
        P("row", "col"),
        P(("row", "col"), None),
        P(None, ("row", "col")),
        P(),
        P(),
        P(),
    )
    out_specs = P(("row", "col"), None)
    return jax.shard_map(
        on_device, mesh=mesh, in_specs=in_specs, out_specs=out_specs, check_vma=False
    )
```
